512 devices in a mesh: rep: 4 (over x), fsdp: 16 (over z), tp: 8 (over y, core).
Axes of the slice: x: 4, y: 4, z: 16, core: 2. Of those that a mesh axis runs over, the one named last changes fastest.
Arguments:
- tracker: bfloat16 [4, 4096, 14336], P('rep', 'fsdp', 'tp'), may hold values from -20 to 20
- grad_delta: bfloat16 [4, 4096, 14336], P('rep', 'fsdp', 'tp'), may hold values from -20 to 20
- momentum: bfloat16 [4, 4096, 14336], P('rep', 'fsdp', 'tp'), may hold values from -20 to 20
- q_basis: bfloat16 [4, 14336, 512], P('rep', 'tp', 'fsdp'), may hold values from -0.046875 to 0.046875
- mix_counts: int32 [4, 3], replicated, may hold values from 1 to 8
Outputs:
- new_tracker: bfloat16 [4, 4096, 14336], P('rep', 'fsdp', 'tp')
- new_momentum: bfloat16 [4, 4096, 14336], P('rep', 'fsdp', 'tp')
- left_basis: bfloat16 [4, 4096, 512], P('rep', 'fsdp')
- q_new: bfloat16 [4, 14336, 512], P('rep', 'tp', 'fsdp')
The draws below stay inside these ranges and needn't reach their ends.
All inputs are finite; a program needn't handle non-finite values.
Results may differ from the reference program's by a relative error of at most 0.0061.
Values may be sent and summed in bfloat16 or wider, within the bound.
A program may use at most 64 MiB of HBM per device.

```python
import math
import jax
import jax.numpy as jnp
from jax import lax

D = 4096
FF = 14336
RANK = 512
AGENTS = 4


def profile(key):
    inner = jax.random.fold_in(key, 9173)
    key_rows, key_cols = jax.random.split(inner)
    spread = 0.6
    rise_rows = jnp.arange(D, dtype=jnp.float32) / D
    rise_cols = jnp.arange(FF, dtype=jnp.float32) / FF
    noise_rows = jax.random.uniform(key_rows, (D,), jnp.float32)
    noise_cols = jax.random.uniform(key_cols, (FF,), jnp.float32)
    row_scale = jnp.exp(math.log(3.0) * rise_rows + spread * noise_rows)
    col_scale = jnp.exp(math.log(3.0) * rise_cols + spread * noise_cols)
    return (row_scale, col_scale)


def scaled_field(key, salt, factor):
    row_scale, col_scale = profile(key)
    own = jax.random.fold_in(key, salt)
    base = jnp.clip(jax.random.normal(own, (AGENTS, D, FF), jnp.float32), -4.0, 4.0)
    return (factor * base * row_scale[None, :, None] * col_scale[None, None, :]).astype(jnp.bfloat16)


def draw_tracker(key, part):
    return scaled_field(key, 11, 0.15)


def draw_grad_delta(key, part):
    return scaled_field(key, 23, 0.08)


def draw_momentum(key, part):
    return scaled_field(key, 37, 0.15)


def place_ends(entries, own_key, least, largest):
    longest = entries.shape.index(max(entries.shape))
    spots = []
    for shift in (0, 1):
        where = [jax.random.randint(jax.random.fold_in(own_key, axis), (), 0, length) for axis, length in enumerate(entries.shape)]
        where[longest] = (where[longest] + shift) % entries.shape[longest]
        spots.append(tuple(where))
    return entries.at[spots[0]].set(least).at[spots[1]].set(largest)


def shard_levels(own_key, shape, cuts, smallest, top_value):
    loudness = 1.0
    for position, parts in cuts:
        draws = jax.random.uniform(jax.random.fold_in(jax.random.fold_in(own_key, 6), position), (parts,), jnp.float32, smallest / len(cuts), top_value / len(cuts))
        loudness = loudness * jnp.repeat(jnp.exp(draws), shape[position] // parts).reshape((-1,) + (1,) * (len(shape) - 1 - position))
    return loudness


def gaussian(stream_key, shape, scale, reach, pieces=(), kind=jnp.bfloat16):
    drawn = jax.random.normal(stream_key, shape, jnp.float32) * scale
    if len(pieces) > 0:
        drawn = shard_levels(stream_key, shape, pieces, -0.22, 0.18) * drawn
    return jnp.clip(drawn, min=-reach, max=reach).astype(kind)


def setup_inputs(seed: int = 0) -> dict:
    key_list = jax.random.split(jax.random.key(seed), 6)
    tracker = draw_tracker(jax.random.fold_in(key_list[5], 71), 0)
    grad_delta = draw_grad_delta(jax.random.fold_in(key_list[5], 71), 0)
    momentum = draw_momentum(jax.random.fold_in(key_list[5], 71), 0)
    q_basis = gaussian(key_list[3], (AGENTS, FF, RANK), FF ** -0.5, 0.046875, ((0, 4), (1, 8), (2, 16)))
    mix_counts = place_ends(jax.random.randint(key_list[4], (AGENTS, 3), 1, 9), jax.random.fold_in(key_list[4], 1), 1, 8).astype(jnp.int32)
    return dict(tracker=tracker, grad_delta=grad_delta, momentum=momentum, q_basis=q_basis, mix_counts=mix_counts)


def reference(tracker, grad_delta, momentum, q_basis, mix_counts):
    counts = mix_counts.astype(jnp.float32)
    weights = counts / lax.optimization_barrier(jnp.sum(counts, axis=1, keepdims=True))
    scale = 1.0 / jnp.sqrt(jnp.float32(D))
    out_tracker = []
    out_momentum = []
    out_left = []
    out_right = []
    for agent in range(AGENTS):
        before = (agent - 1) % AGENTS
        after = (agent + 1) % AGENTS
        mixed = weights[agent, 0] * tracker[agent].astype(jnp.float32) + weights[agent, 1] * tracker[before].astype(jnp.float32) + weights[agent, 2] * tracker[after].astype(jnp.float32)
        tracked = mixed + grad_delta[agent].astype(jnp.float32)
        out_tracker.append(tracked.astype(jnp.bfloat16))
        accum = momentum[agent].astype(jnp.float32) + tracked
        accum_b = accum.astype(jnp.bfloat16)
        pmat = jnp.dot(accum_b.astype(jnp.float32), q_basis[agent].astype(jnp.float32), preferred_element_type=jnp.float32)
        gram = jnp.dot(pmat.T, pmat, precision=lax.Precision.HIGHEST)
        chol = jnp.linalg.cholesky(gram)
        left = jax.scipy.linalg.solve_triangular(chol, pmat.T, lower=True).T * jnp.sqrt(jnp.float32(D))
        left_b = left.astype(jnp.bfloat16)
        out_left.append(left_b)
        right = jnp.dot(accum_b.T.astype(jnp.float32), left_b.astype(jnp.float32), preferred_element_type=jnp.float32) * scale
        rms = jnp.sqrt(lax.optimization_barrier(jnp.mean(right * right, axis=0))) + 1e-06
        out_right.append((right / rms[None, :]).astype(jnp.bfloat16))
        right_b = right.astype(jnp.bfloat16)
        feed = jnp.dot(left_b.astype(jnp.float32), right_b.T.astype(jnp.float32), preferred_element_type=jnp.float32)
        out_momentum.append((accum - 0.5 * scale * feed).astype(jnp.bfloat16))
    return (jnp.stack(out_tracker), jnp.stack(out_momentum), jnp.stack(out_left), jnp.stack(out_right))
```

```python
import jax
import jax.numpy as jnp
from jax import lax
from jax.experimental import pallas as pl
from jax.experimental.pallas import tpu as pltpu
from jax.sharding import PartitionSpec as P

D = 4096
FF = 14336


def extended(block, sides, width):
    for axis, dim in sides:
        count = lax.axis_size(axis)
        forward = [(i, i + 1) for i in range(count - 1)]
        forward.append((count - 1, 0))
        backward = [(target, source) for source, target in forward]
        low = lax.ppermute(
            lax.slice_in_dim(block, block.shape[dim] - width, None, axis=dim), axis, forward
        )
        high = lax.ppermute(lax.slice_in_dim(block, 0, width, axis=dim), axis, backward)
        block = jnp.concatenate([low, block, high], axis=dim)
    return block


NB = 128
HI = lax.Precision.HIGHEST

def factor_inverse(load, store):
    G = NB // 8
    sub = lax.broadcasted_iota(jnp.int32, (8, NB), 0)
    lane = lax.broadcasted_iota(jnp.int32, (8, NB), 1)
    A = [load(h) for h in range(G)]
    W = [jnp.where(lane == sub + 8 * h, 1.0, 0.0).astype(jnp.float32) for h in range(G)]
    row = lambda x, a: jnp.broadcast_to(x[a:a + 1, :], (8, NB))
    colb = lambda x, j: jnp.broadcast_to(x[:, j:j + 1], (8, NB))
    for g in range(G):
        j0 = 8 * g
        RA, RW = A[g], W[g]
        E = [colb(RA, j0 + a) for a in range(8)]
        FA, FW = RA, RW
        for a in range(8):
            ra, rw = row(RA, a), row(RW, a)
            inv = 1.0 / row(E[a], a)
            hit = sub == a
            FA = jnp.where(hit, ra, FA)
            FW = jnp.where(hit, rw, FW)
            sa, sw = ra * inv, rw * inv
            RA = jnp.where(hit, sa, RA - E[a] * sa)
            RW = jnp.where(hit, sw, RW - E[a] * sw)
            for b in range(a + 1, 8):
                eb = row(E[b], a) * inv
                E[b] = jnp.where(hit, eb, E[b] - E[a] * eb)
        A[g], W[g] = FA, FW
        SA = [row(RA, a) for a in range(8)]
        SW = [row(RW, a) for a in range(8)]
        for h in range(g + 1, G):
            ah, wh, src = A[h], W[h], A[h]
            for a in range(8):
                c = colb(src, j0 + a)
                ah = ah - c * SA[a]
                wh = wh - c * SW[a]
            A[h], W[h] = ah, wh
    for g in range(G):
        d = jnp.sum(jnp.where(lane == sub + 8 * g, A[g], 0.0), axis=1, keepdims=True)
        store(g, W[g] * lax.rsqrt(d))

def nt(a, b):
    return lax.dot_general(a, b, (((1,), (1,)), ((), ())), precision=HI, preferred_element_type=jnp.float32)

def solve_kernel(g_ref, p_ref, o_ref, t_ref, w_ref):
    n = g_ref.shape[0]
    m = p_ref.shape[0]
    K = n // NB
    t_ref[0:n, :] = g_ref[...]
    t_ref[n:n + m, :] = p_ref[...]
    def step(k, _):
        base = pl.multiple_of(k * NB, NB)
        def load(h):
            return t_ref[pl.ds(pl.multiple_of(base + 8 * h, 8), 8), pl.ds(base, NB)]
        def store(h, v):
            w_ref[8 * h:8 * h + 8, :] = v
        factor_inverse(load, store)
        for kk in range(K):
            @pl.when(k == kk)
            def _():
                lo, hi = kk * NB, (kk + 1) * NB
                x = nt(t_ref[hi:, lo:hi], w_ref[...])
                o_ref[:, lo:hi] = (x[n - hi:] * D ** 0.5).astype(jnp.bfloat16)
                if kk + 1 < K:
                    t_ref[hi:, hi:] = t_ref[hi:, hi:] - nt(x, x[:n - hi])
        return 0
    lax.fori_loop(0, K, step, 0)

def left_solve(gram, pmat):
    n, m = gram.shape[0], pmat.shape[0]
    return pl.pallas_call(
        solve_kernel,
        out_shape=jax.ShapeDtypeStruct((m, n), jnp.bfloat16),
        in_specs=[pl.BlockSpec(memory_space=pltpu.VMEM)] * 2,
        out_specs=pl.BlockSpec(memory_space=pltpu.VMEM),
        scratch_shapes=[pltpu.VMEM((n + m, n), jnp.float32), pltpu.VMEM((NB, NB), jnp.float32)],
        compiler_params=pltpu.CompilerParams(vmem_limit_bytes=40 << 20),
    )(gram, pmat)


def local(tracker, grad_delta, momentum, q_basis, mix_counts):
    agent = lax.axis_index("rep")
    counts = mix_counts.astype(jnp.float32)
    select = (jnp.arange(counts.shape[0]) == agent).astype(jnp.float32)
    mine = jnp.sum(select[:, None] * counts, axis=0)
    weights = mine / jnp.sum(mine)
    near = extended(tracker, (("rep", 0),), 1)
    mixed = (
        weights[0] * near[1].astype(jnp.float32)
        + weights[1] * near[0].astype(jnp.float32)
        + weights[2] * near[2].astype(jnp.float32)
    )
    tracked = mixed + grad_delta[0].astype(jnp.float32)
    new_tracker = tracked.astype(jnp.bfloat16)
    accum = momentum[0].astype(jnp.float32) + tracked
    accum_b = accum.astype(jnp.bfloat16)
    scale = 1.0 / jnp.sqrt(jnp.float32(D))
    basis_full = lax.all_gather(q_basis, "fsdp", axis=2, tiled=True)[0]
    partial_left = jnp.dot(accum_b, basis_full, preferred_element_type=jnp.float32)
    pmat = lax.psum(partial_left, "tp")
    gram_part = jnp.dot(pmat.T, pmat, precision=lax.Precision.HIGHEST)
    gram = lax.psum(gram_part, "fsdp")
    left_b = left_solve(gram, pmat)
    block = left_b
    product = lax.dot_general(
        block, accum_b, (((0,), (0,)), ((), ())), preferred_element_type=jnp.float32
    )
    right_t = lax.psum_scatter(product * scale, "fsdp", scatter_dimension=0, tiled=True)
    squares = lax.psum(jnp.sum(right_t * right_t, axis=1), "tp")
    rms = jnp.sqrt(squares / FF) + 1e-06
    q_new = (right_t / rms[:, None]).T.astype(jnp.bfloat16)
    right_b = right_t.astype(jnp.bfloat16)
    block = left_b
    feed = jnp.dot(
        block,
        lax.all_gather(right_b, "fsdp", axis=0, tiled=True),
        preferred_element_type=jnp.float32,
    )
    new_momentum = (accum - 0.5 * scale * feed).astype(jnp.bfloat16)
    return (new_tracker[None], new_momentum[None], left_b[None], q_new[None])


def solution(mesh):
    in_specs = (
        P("rep", "fsdp", "tp"),
        P("rep", "fsdp", "tp"),
        P("rep", "fsdp", "tp"),
        P("rep", "tp", "fsdp"),
        P(),
    )
    out_specs = (
        P("rep", "fsdp", "tp"),
        P("rep", "fsdp", "tp"),
        P("rep", "fsdp", None),
        P("rep", "tp", "fsdp"),
    )
    return jax.shard_map(local, mesh=mesh, in_specs=in_specs, out_specs=out_specs, check_vma=False)
```

```python
import jax
import jax.numpy as jnp
from jax import lax
from jax.experimental import pallas as pl
from jax.experimental.pallas import tpu as pltpu
from jax.sharding import PartitionSpec as P

D = 4096
FF = 14336


NB = 128
HI = lax.Precision.HIGHEST

def factor_inverse(load, store):
    G = NB // 8
    sub = lax.broadcasted_iota(jnp.int32, (8, NB), 0)
    lane = lax.broadcasted_iota(jnp.int32, (8, NB), 1)
    A = [load(h) for h in range(G)]
    W = [jnp.where(lane == sub + 8 * h, 1.0, 0.0).astype(jnp.float32) for h in range(G)]
    row = lambda x, a: jnp.broadcast_to(x[a:a + 1, :], (8, NB))
    colb = lambda x, j: jnp.broadcast_to(x[:, j:j + 1], (8, NB))
    for g in range(G):
        j0 = 8 * g
        RA, RW = A[g], W[g]
        E = [colb(RA, j0 + a) for a in range(8)]
        FA, FW = RA, RW
        for a in range(8):
            ra, rw = row(RA, a), row(RW, a)
            inv = 1.0 / row(E[a], a)
            hit = sub == a
            FA = jnp.where(hit, ra, FA)
            FW = jnp.where(hit, rw, FW)
            sa, sw = ra * inv, rw * inv
            RA = jnp.where(hit, sa, RA - E[a] * sa)
            RW = jnp.where(hit, sw, RW - E[a] * sw)
            for b in range(a + 1, 8):
                eb = row(E[b], a) * inv
                E[b] = jnp.where(hit, eb, E[b] - E[a] * eb)
        A[g], W[g] = FA, FW
        SA = [row(RA, a) for a in range(8)]
        SW = [row(RW, a) for a in range(8)]
        for h in range(g + 1, G):
            ah, wh, src = A[h], W[h], A[h]
            for a in range(8):
                c = colb(src, j0 + a)
                ah = ah - c * SA[a]
                wh = wh - c * SW[a]
            A[h], W[h] = ah, wh
    for g in range(G):
        d = jnp.sum(jnp.where(lane == sub + 8 * g, A[g], 0.0), axis=1, keepdims=True)
        store(g, W[g] * lax.rsqrt(d))

def nt(a, b):
    return lax.dot_general(a, b, (((1,), (1,)), ((), ())), precision=HI, preferred_element_type=jnp.float32)

def solve_kernel(g_ref, p_ref, o_ref, t_ref, w_ref):
    n = g_ref.shape[0]
    m = p_ref.shape[0]
    K = n // NB
    t_ref[0:n, :] = g_ref[...]
    t_ref[n:n + m, :] = p_ref[...]
    def step(k, _):
        base = pl.multiple_of(k * NB, NB)
        def load(h):
            return t_ref[pl.ds(pl.multiple_of(base + 8 * h, 8), 8), pl.ds(base, NB)]
        def store(h, v):
            w_ref[8 * h:8 * h + 8, :] = v
        factor_inverse(load, store)
        for kk in range(K):
            @pl.when(k == kk)
            def _():
                lo, hi = kk * NB, (kk + 1) * NB
                x = nt(t_ref[hi:, lo:hi], w_ref[...])
                o_ref[:, lo:hi] = (x[n - hi:] * D ** 0.5).astype(jnp.bfloat16)
                if kk + 1 < K:
                    t_ref[hi:, hi:] = t_ref[hi:, hi:] - nt(x, x[:n - hi])
        return 0
    lax.fori_loop(0, K, step, 0)

def left_solve(gram, pmat):
    n, m = gram.shape[0], pmat.shape[0]
    return pl.pallas_call(
        solve_kernel,
        out_shape=jax.ShapeDtypeStruct((m, n), jnp.bfloat16),
        in_specs=[pl.BlockSpec(memory_space=pltpu.VMEM)] * 2,
        out_specs=pl.BlockSpec(memory_space=pltpu.VMEM),
        scratch_shapes=[pltpu.VMEM((n + m, n), jnp.float32), pltpu.VMEM((NB, NB), jnp.float32)],
        compiler_params=pltpu.CompilerParams(vmem_limit_bytes=40 << 20),
    )(gram, pmat)


MESH = pl.DeviceIdType.MESH
Z, Y, T = 16, 4, 8
BF = jnp.bfloat16
F32 = jnp.float32


def ds(start, size):
    return pl.ds(pl.multiple_of(start, size), size)


def push(src, dst, ssem, rsem, **where):
    copy = pltpu.make_async_remote_copy(
        src_ref=src, dst_ref=dst, send_sem=ssem, recv_sem=rsem, device_id=where, device_id_type=MESH
    )
    copy.start()
    return copy


def enter(peers):
    barrier = pltpu.get_barrier_semaphore()
    for where in peers:
        pl.semaphore_signal(barrier, inc=1, device_id=where, device_id_type=MESH)
    pl.semaphore_wait(barrier, len(peers))


def ring_gather(first, full, ssem, rsem):
    me = lax.axis_index("fsdp")
    right, left = lax.rem(me + 1, Z), lax.rem(me + Z - 1, Z)
    sent = []
    last = {}
    for s in range(Z // 2):
        for h in range(2):
            for way in range(2):
                if way == 1 and s == Z // 2 - 1:
                    continue
                owner = lax.rem(me - s + Z, Z) if way == 0 else lax.rem(me + s, Z)
                dst = full.at[ds(owner * 32 + 16 * h, 16), :]
                if s > 0:
                    last[h, way].wait_recv()
                src = first.at[16 * h:16 * h + 16, :] if s == 0 else dst
                copy = push(src, dst, ssem.at[way, s, h], rsem.at[way, s, h], fsdp=right if way == 0 else left)
                last[h, way] = copy
                sent.append(copy)
    for copy in last.values():
        copy.wait_recv()
    return sent


def y_gather(view, partner_too, ssem, rsem, psend, precv):
    tp = lax.axis_index("tp")
    y, core = tp // 2, lax.rem(tp, 2)
    other = tp + 1 - 2 * core
    up, down, far = lax.rem(y + 1, Y), lax.rem(y + Y - 1, Y), lax.rem(y + 2, Y)
    sent = []
    cross = []
    halves = {}
    for h in range(2):
        for way, goal in ((0, up), (1, down)):
            copy = push(view(y, core, h), view(y, core, h), ssem.at[way, h], rsem.at[way, h], tp=goal * 2 + core)
            halves[way, h] = copy
            sent.append(copy)
    for h in range(2):
        cross.append(push(view(y, core, h), view(y, core, h), psend.at[0, h], precv.at[0, h], tp=other))
    for h in (0, 1):
        way = h
        origin, goal = (down, up) if way == 0 else (up, down)
        halves[way, h].wait_recv()
        copy = push(view(origin, core, h), view(origin, core, h), ssem.at[2, h], rsem.at[2, h], tp=goal * 2 + core)
        halves[2, h] = copy
        sent.append(copy)
        cross.append(push(view(origin, core, h), view(origin, core, h), psend.at[1 + way, h], precv.at[1 + way, h], tp=other))
    for way, h in ((0, 1), (1, 0)):
        origin = down if way == 0 else up
        halves[way, h].wait_recv()
        cross.append(push(view(origin, core, h), view(origin, core, h), psend.at[1 + way, h], precv.at[1 + way, h], tp=other))
    for h in range(2):
        halves[2, h].wait_recv()
        cross.append(push(view(far, core, h), view(far, core, h), psend.at[3, h], precv.at[3, h], tp=other))
    for copy in cross:
        copy.wait_recv()
    return sent + cross


def front_kernel(mix_ref, tr_ref, gd_ref, mo_ref, q_ref, nt_ref, ab_ref, ac_ref, p_ref, g_ref,
                 tlo, thi, qfull, part, rx1, half, rx2, own, gw, gp, rg,
                 xs, xr, qs, qr, cs, cr, ys, yr, ags, agr, aps, apr, zs, zr, gs, gr, hs, hr, hps, hpr):
    x = lax.axis_index("rep")
    z = lax.axis_index("fsdp")
    tp = lax.axis_index("tp")
    y, core = tp // 2, lax.rem(tp, 2)
    other = tp + 1 - 2 * core
    xn = lax.axis_size("rep")
    xu, xd = lax.rem(x + 1, xn), lax.rem(x + xn - 1, xn)
    zu, zd = lax.rem(z + 1, Z), lax.rem(z + Z - 1, Z)
    ypeers = [lax.rem(y + d, Y) * 2 + core for d in range(1, Y)]
    enter([{"rep": xu}, {"rep": xd}, {"fsdp": zu}, {"fsdp": zd}, {"tp": other}] + [{"tp": t} for t in ypeers])
    sent = []
    up = push(tr_ref, tlo, xs.at[0], xr.at[0], rep=xu)
    down = push(tr_ref, thi, xs.at[1], xr.at[1], rep=xd)
    sent += [up, down]
    qfull[ds(z * 32, 32), :] = q_ref[...]
    sent += ring_gather(q_ref, qfull, qs, qr)
    up.wait_recv()
    down.wait_recv()
    c = [jnp.full((8, 128), mix_ref[x, i].astype(F32)) for i in range(3)]
    total = c[0] + c[1] + c[2]
    w = [(v / total)[0:1, 0:1] for v in c]

    def mixing(i, _):
        r = ds(i * 16, 16)
        tracked = (
            w[0] * tr_ref[r, :].astype(F32) + w[1] * tlo[r, :].astype(F32) + w[2] * thi[r, :].astype(F32)
        ) + gd_ref[r, :].astype(F32)
        accum = mo_ref[r, :].astype(F32) + tracked
        nt_ref[r, :] = tracked.astype(BF)
        ac_ref[r, :] = accum
        ab_ref[r, :] = accum.astype(BF)
        return 0

    lax.fori_loop(0, tr_ref.shape[0] // 16, mixing, 0)
    for n in range(2):
        part[:, 256 * n:256 * n + 256] = lax.dot_general(
            ab_ref[...], qfull[256 * n:256 * n + 256, :], (((1,), (1,)), ((), ())), preferred_element_type=F32
        )
    swap = push(part.at[ds((1 - core) * 128, 128), :], rx1, cs, cr, tp=other)
    sent.append(swap)
    swap.wait_recv()
    half[...] = part[ds(core * 128, 128), :] + rx1[...]
    shares = []
    for d in range(1, Y):
        yd = lax.rem(y + d, Y)
        shares.append(push(half.at[ds(yd * 32, 32), :], rx2.at[d - 1], ys.at[d - 1], yr.at[d - 1], tp=yd * 2 + core))
    sent += shares
    for copy in shares:
        copy.wait_recv()
    p_ref[ds(core * 128 + y * 32, 32), :] = ((half[ds(y * 32, 32), :] + rx2[0]) + rx2[1]) + rx2[2]

    def pview(yy, cc, h):
        return p_ref.at[ds(cc * 128 + yy * 32 + 16 * h, 16), :]

    sent += y_gather(pview, True, ags, agr, aps, apr)
    gw[...] = lax.dot_general(
        p_ref[:, ds(y * 128, 128)], p_ref[...], (((0,), (0,)), ((), ())), precision=HI, preferred_element_type=F32
    )
    gp[...] = gw[ds(core * 64, 64), :]

    def piece(ref, base, zz):
        return ref.at[ds(base + 8 * (zz // 2), 8), ds(256 * lax.rem(zz, 2), 256)]

    pieces = []
    for d in range(1, Z):
        zz = lax.rem(z + d, Z)
        pieces.append(push(piece(gp, 0, zz), rg.at[d - 1], zs.at[d - 1], zr.at[d - 1], fsdp=zz))
    sent += pieces
    acc = gp[ds(8 * (z // 2), 8), ds(256 * lax.rem(z, 2), 256)]
    for d in range(1, Z):
        pieces[d - 1].wait_recv()
        acc = acc + rg[d - 1]
    base = y * 128 + core * 64
    g_ref[ds(base + 8 * (z // 2), 8), ds(256 * lax.rem(z, 2), 256)] = acc
    out = []
    for d in range(1, Z):
        zz = lax.rem(z + d, Z)
        out.append(push(piece(g_ref, base, z), piece(g_ref, base, z), gs.at[d - 1], gr.at[d - 1], fsdp=zz))
    sent += out
    for copy in out:
        copy.wait_recv()

    def gview(yy, cc, h):
        return g_ref.at[ds(yy * 128 + cc * 64 + 32 * h, 32), :]

    sent += y_gather(gview, True, hs, hr, hps, hpr)
    for copy in sent:
        copy.wait_send()


VM = pl.BlockSpec(memory_space=pltpu.VMEM)
DMA = pltpu.SemaphoreType.DMA


def front(mix, tracker, grad, momentum, q_t):
    rows, cols = tracker.shape
    rank = q_t.shape[0] * Z
    sd = jax.ShapeDtypeStruct
    vm = pltpu.VMEM
    return pl.pallas_call(
        front_kernel,
        out_shape=(sd((rows, cols), BF), sd((rows, cols), BF), sd((rows, cols), F32), sd((rows, rank), F32), sd((rank, rank), F32)),
        in_specs=[pl.BlockSpec(memory_space=pltpu.SMEM)] + [VM] * 4,
        out_specs=(VM,) * 5,
        scratch_shapes=[
            vm((rows, cols), BF), vm((rows, cols), BF), vm((rank, cols), BF), vm((rows, rank), F32),
            vm((128, rank), F32), vm((128, rank), F32), vm((3, 32, rank), F32), vm((32, rank), F32),
            vm((128, rank), F32), vm((64, rank), F32), vm((15, 8, 256), F32),
            DMA((2,)), DMA((2,)), DMA((2, 8, 2)), DMA((2, 8, 2)), DMA, DMA, DMA((3,)), DMA((3,)),
            DMA((3, 2)), DMA((3, 2)), DMA((4, 2)), DMA((4, 2)),
            DMA((15,)), DMA((15,)), DMA((15,)), DMA((15,)),
            DMA((3, 2)), DMA((3, 2)), DMA((4, 2)), DMA((4, 2)),
        ],
        compiler_params=pltpu.CompilerParams(collective_id=0, has_side_effects=True, vmem_limit_bytes=48 << 20),
    )(mix, tracker, grad, momentum, q_t)


def back_kernel(lb_ref, ab_ref, ac_ref, qn_ref, nm_ref, prod, sbuf, rbuf, rb, rfull, sq, sqr,
                rs, rr, gs, gr, ss, sr):
    me = lax.axis_index("fsdp")
    tp = lax.axis_index("tp")
    right, left = lax.rem(me + 1, Z), lax.rem(me + Z - 1, Z)
    peers = [lax.rem(tp + d, T) for d in range(1, T)]
    enter([{"fsdp": right}, {"fsdp": left}] + [{"tp": t} for t in peers])
    cols = ab_ref.shape[1]
    scale = 1.0 / D ** 0.5
    for n in range(cols // 256):
        prod[:, 256 * n:256 * n + 256] = lax.dot_general(
            lb_ref[...], ab_ref[:, 256 * n:256 * n + 256], (((0,), (0,)), ((), ())), preferred_element_type=F32
        ) * scale
    sent = []
    last = {}
    for s in range(Z // 2):
        for h in range(2):
            for way in range(2):
                if way == 0 and s == Z // 2 - 1:
                    continue
                goal = lax.rem(me + 7 - s, Z) if way == 0 else lax.rem(me + Z - 8 + s, Z)
                term = prod[ds(goal * 32 + 16 * h, 16), :]
                if s > 0:
                    last[h, way].wait_recv()
                    term = term + rbuf[way, s - 1, 16 * h:16 * h + 16, :].astype(F32)
                sbuf[way, s, 16 * h:16 * h + 16, :] = term.astype(BF)
                copy = push(
                    sbuf.at[way, s, 16 * h:16 * h + 16, :], rbuf.at[way, s, 16 * h:16 * h + 16, :],
                    rs.at[way, s, h], rr.at[way, s, h], fsdp=right if way == 0 else left,
                )
                last[h, way] = copy
                sent.append(copy)
    for copy in last.values():
        copy.wait_recv()
    mine = prod[ds(me * 32, 32), :] + rbuf[0, 6].astype(F32) + rbuf[1, 7].astype(F32)
    rb[...] = mine.astype(BF)
    rfull[ds(me * 32, 32), :] = mine.astype(BF)
    sq[...] = jnp.broadcast_to(jnp.sum(mine * mine, axis=1, keepdims=True), sq.shape)
    small = []
    for d in range(1, T):
        small.append(push(sq, sqr.at[d - 1], ss.at[d - 1], sr.at[d - 1], tp=peers[d - 1]))
    sent += small
    sent += ring_gather(rb, rfull, gs, gr)
    total = sq[...]
    for d in range(1, T):
        small[d - 1].wait_recv()
        total = total + sqr[d - 1]
    rms = jnp.sqrt(total / FF) + 1e-06
    qn_ref[...] = (mine / rms[:, 0:1]).astype(BF)
    for n in range(cols // 256):
        part = slice(256 * n, 256 * n + 256)
        feed = jnp.dot(lb_ref[...], rfull[:, part], preferred_element_type=F32)
        nm_ref[:, part] = (ac_ref[:, part] - 0.5 * scale * feed).astype(BF)
    for copy in sent:
        copy.wait_send()


def back(left_b, accum_b, accum):
    rows, cols = accum.shape
    rank = left_b.shape[1]
    sd = jax.ShapeDtypeStruct
    vm = pltpu.VMEM
    return pl.pallas_call(
        back_kernel,
        out_shape=(sd((32, cols), BF), sd((rows, cols), BF)),
        in_specs=[VM] * 3,
        out_specs=(VM,) * 2,
        scratch_shapes=[
            vm((rank, cols), F32), vm((2, 8, 32, cols), BF), vm((2, 8, 32, cols), BF), vm((32, cols), BF),
            vm((rank, cols), BF), vm((32, 128), F32), vm((7, 32, 128), F32),
            DMA((2, 8, 2)), DMA((2, 8, 2)), DMA((2, 8, 2)), DMA((2, 8, 2)), DMA((7,)), DMA((7,)),
        ],
        compiler_params=pltpu.CompilerParams(collective_id=1, has_side_effects=True, vmem_limit_bytes=48 << 20),
    )(left_b, accum_b, accum)


def local(tracker, grad_delta, momentum, q_basis, mix_counts):
    new_tracker, accum_b, accum, pmat, gram = front(mix_counts, tracker[0], grad_delta[0], momentum[0], q_basis[0].T)
    left_b = left_solve(gram, pmat)
    q_t, new_momentum = back(left_b, accum_b, accum)
    return (new_tracker[None], new_momentum[None], left_b[None], q_t.T[None])


def solution(mesh):
    in_specs = (
        P("rep", "fsdp", "tp"),
        P("rep", "fsdp", "tp"),
        P("rep", "fsdp", "tp"),
        P("rep", "tp", "fsdp"),
        P(),
    )
    out_specs = (
        P("rep", "fsdp", "tp"),
        P("rep", "fsdp", "tp"),
        P("rep", "fsdp", None),
        P("rep", "tp", "fsdp"),
    )
    return jax.shard_map(local, mesh=mesh, in_specs=in_specs, out_specs=out_specs, check_vma=False)
```

```python
import jax
import jax.numpy as jnp
from jax import lax
from jax.experimental import pallas as pl
from jax.experimental.pallas import tpu as pltpu
from jax.sharding import PartitionSpec as P

D = 4096
FF = 14336


NB = 128
HI = lax.Precision.HIGHEST

def factor_inverse(load, store):
    G = NB // 8
    sub = lax.broadcasted_iota(jnp.int32, (8, NB), 0)
    lane = lax.broadcasted_iota(jnp.int32, (8, NB), 1)
    A = [load(h) for h in range(G)]
    W = [jnp.where(lane == sub + 8 * h, 1.0, 0.0).astype(jnp.float32) for h in range(G)]
    row = lambda x, a: jnp.broadcast_to(x[a:a + 1, :], (8, NB))
    colb = lambda x, j: jnp.broadcast_to(x[:, j:j + 1], (8, NB))
    for g in range(G):
        j0 = 8 * g
        RA, RW = A[g], W[g]
        E = [colb(RA, j0 + a) for a in range(8)]
        FA, FW = RA, RW
        for a in range(8):
            ra, rw = row(RA, a), row(RW, a)
            inv = 1.0 / row(E[a], a)
            hit = sub == a
            FA = jnp.where(hit, ra, FA)
            FW = jnp.where(hit, rw, FW)
            sa, sw = ra * inv, rw * inv
            RA = jnp.where(hit, sa, RA - E[a] * sa)
            RW = jnp.where(hit, sw, RW - E[a] * sw)
            for b in range(a + 1, 8):
                eb = row(E[b], a) * inv
                E[b] = jnp.where(hit, eb, E[b] - E[a] * eb)
        A[g], W[g] = FA, FW
        SA = [row(RA, a) for a in range(8)]
        SW = [row(RW, a) for a in range(8)]
        for h in range(g + 1, G):
            ah, wh, src = A[h], W[h], A[h]
            for a in range(8):
                c = colb(src, j0 + a)
                ah = ah - c * SA[a]
                wh = wh - c * SW[a]
            A[h], W[h] = ah, wh
    for g in range(G):
        d = jnp.sum(jnp.where(lane == sub + 8 * g, A[g], 0.0), axis=1, keepdims=True)
        store(g, W[g] * lax.rsqrt(d))

def nt(a, b):
    return lax.dot_general(a, b, (((1,), (1,)), ((), ())), precision=HI, preferred_element_type=jnp.float32)

def solve_kernel(g_ref, p_ref, o_ref, t_ref, w_ref):
    n = g_ref.shape[0]
    m = p_ref.shape[0]
    K = n // NB
    t_ref[0:n, :] = g_ref[...]
    t_ref[n:n + m, :] = p_ref[...]
    def step(k, _):
        base = pl.multiple_of(k * NB, NB)
        def load(h):
            return t_ref[pl.ds(pl.multiple_of(base + 8 * h, 8), 8), pl.ds(base, NB)]
        def store(h, v):
            w_ref[8 * h:8 * h + 8, :] = v
        factor_inverse(load, store)
        for kk in range(K):
            @pl.when(k == kk)
            def _():
                lo, hi = kk * NB, (kk + 1) * NB
                x = nt(t_ref[hi:, lo:hi], w_ref[...])
                o_ref[:, lo:hi] = (x[n - hi:] * D ** 0.5).astype(jnp.bfloat16)
                if kk + 1 < K:
                    t_ref[hi:, hi:] = t_ref[hi:, hi:] - nt(x, x[:n - hi])
        return 0
    lax.fori_loop(0, K, step, 0)

def left_solve(gram, pmat):
    n, m = gram.shape[0], pmat.shape[0]
    return pl.pallas_call(
        solve_kernel,
        out_shape=jax.ShapeDtypeStruct((m, n), jnp.bfloat16),
        in_specs=[pl.BlockSpec(memory_space=pltpu.VMEM)] * 2,
        out_specs=pl.BlockSpec(memory_space=pltpu.VMEM),
        scratch_shapes=[pltpu.VMEM((n + m, n), jnp.float32), pltpu.VMEM((NB, NB), jnp.float32)],
        compiler_params=pltpu.CompilerParams(vmem_limit_bytes=67043328),
    )(gram, pmat)


MESH = pl.DeviceIdType.MESH
Z, Y, T = 16, 4, 8
BF = jnp.bfloat16
F32 = jnp.float32


def ds(start, size):
    return pl.ds(pl.multiple_of(start, size), size)


def push(src, dst, ssem, rsem, **where):
    copy = pltpu.make_async_remote_copy(
        src_ref=src, dst_ref=dst, send_sem=ssem, recv_sem=rsem, device_id=where, device_id_type=MESH
    )
    copy.start()
    return copy


def enter(peers):
    barrier = pltpu.get_barrier_semaphore()
    for where in peers:
        pl.semaphore_signal(barrier, inc=1, device_id=where, device_id_type=MESH)
    pl.semaphore_wait(barrier, len(peers))


def ring_gather(first, full, ssem, rsem, between=None):
    me = lax.axis_index("fsdp")
    right, left = lax.rem(me + 1, Z), lax.rem(me + Z - 1, Z)
    wide = first.shape[1] // 2
    sent = []
    last = {}
    for s in range(Z // 2):
        for q in range(4):
            h, lanes = q // 2, slice((q % 2) * wide, (q % 2) * wide + wide)
            for way in range(2):
                if s == Z // 2 - 1 and way != h:
                    continue
                owner = lax.rem(me - s + Z, Z) if way == 0 else lax.rem(me + s, Z)
                dst = full.at[ds(owner * 32 + 16 * h, 16), lanes]
                if s > 0:
                    last[q, way].wait_recv()
                src = first.at[16 * h:16 * h + 16, lanes] if s == 0 else dst
                copy = push(src, dst, ssem.at[way, s, q], rsem.at[way, s, q], fsdp=right if way == 0 else left)
                last[q, way] = copy
                sent.append(copy)
        if between is not None:
            between(s)
    for copy in last.values():
        copy.wait_recv()
    return sent


def y_gather(view, partner_too, ssem, rsem, psend, precv):
    tp = lax.axis_index("tp")
    y, core = tp // 2, lax.rem(tp, 2)
    other = tp + 1 - 2 * core
    up, down, far = lax.rem(y + 1, Y), lax.rem(y + Y - 1, Y), lax.rem(y + 2, Y)
    sent = []
    cross = []
    halves = {}
    for h in range(2):
        for way, goal in ((0, up), (1, down)):
            copy = push(view(y, core, h), view(y, core, h), ssem.at[way, h], rsem.at[way, h], tp=goal * 2 + core)
            halves[way, h] = copy
            sent.append(copy)
    for h in range(2):
        cross.append(push(view(y, core, h), view(y, core, h), psend.at[0, h], precv.at[0, h], tp=other))
    for h in (0, 1):
        way = h
        origin, goal = (down, up) if way == 0 else (up, down)
        halves[way, h].wait_recv()
        copy = push(view(origin, core, h), view(origin, core, h), ssem.at[2, h], rsem.at[2, h], tp=goal * 2 + core)
        halves[2, h] = copy
        sent.append(copy)
        cross.append(push(view(origin, core, h), view(origin, core, h), psend.at[1 + way, h], precv.at[1 + way, h], tp=other))
    for way, h in ((0, 1), (1, 0)):
        origin = down if way == 0 else up
        halves[way, h].wait_recv()
        cross.append(push(view(origin, core, h), view(origin, core, h), psend.at[1 + way, h], precv.at[1 + way, h], tp=other))
    for h in range(2):
        halves[2, h].wait_recv()
        cross.append(push(view(far, core, h), view(far, core, h), psend.at[3, h], precv.at[3, h], tp=other))
    for copy in cross:
        copy.wait_recv()
    return sent + cross


def front_kernel(mix_ref, tr_hbm, gd_hbm, mo_hbm, q_ref, nt_ref, ab_hbm, ac_hbm, p_ref, g_ref,
                 tr_ref, gd_ref, mo_ref, ab_ref, ac_ref, lsem, tlo, thi, qfull, part, rx1, half, rx2, own, gw, gp, rg,
                 xs, xr, qs, qr, cs, cr, ys, yr, ags, agr, aps, apr, zs, zr, gs, gr, hs, hr, hps, hpr):
    x = lax.axis_index("rep")
    z = lax.axis_index("fsdp")
    tp = lax.axis_index("tp")
    y, core = tp // 2, lax.rem(tp, 2)
    other = tp + 1 - 2 * core
    xn = lax.axis_size("rep")
    xu, xd = lax.rem(x + 1, xn), lax.rem(x + xn - 1, xn)
    zu, zd = lax.rem(z + 1, Z), lax.rem(z + Z - 1, Z)
    ypeers = [lax.rem(y + d, Y) * 2 + core for d in range(1, Y)]
    loads = [
        pltpu.make_async_copy(src, dst, lsem.at[i])
        for i, (src, dst) in enumerate(((tr_hbm, tr_ref), (gd_hbm, gd_ref), (mo_hbm, mo_ref)))
    ]
    for copy in loads:
        copy.start()
    enter([{"rep": xu}, {"rep": xd}, {"fsdp": zu}, {"fsdp": zd}, {"tp": other}] + [{"tp": t} for t in ypeers])
    sent = []
    arrivals = []
    for k in range(4):
        band = slice(64 * k, 64 * k + 64)
        up = push(tr_hbm.at[band], tlo.at[band], xs.at[0, k], xr.at[0, k], rep=xu)
        down = push(tr_hbm.at[band], thi.at[band], xs.at[1, k], xr.at[1, k], rep=xd)
        arrivals.append((up, down))
        sent += [up, down]
    c = [jnp.full((8, 128), mix_ref[x, i].astype(F32)) for i in range(3)]
    total = c[0] + c[1] + c[2]
    w = [(v / total)[0:1, 0:1] for v in c]

    def mixing(i, _):
        r = ds(i * 16, 16)
        tracked = (
            w[0] * tr_ref[r, :].astype(F32) + w[1] * tlo[r, :].astype(F32) + w[2] * thi[r, :].astype(F32)
        ) + gd_ref[r, :].astype(F32)
        accum = mo_ref[r, :].astype(F32) + tracked
        nt_ref[r, :] = tracked.astype(BF)
        ac_ref[r, :] = accum
        ab_ref[r, :] = accum.astype(BF)
        return 0

    def mix_band(k):
        if k == 0:
            for copy in loads:
                copy.wait()
        for copy in arrivals[k]:
            copy.wait_recv()
        lax.fori_loop(4 * k, 4 * k + 4, mixing, 0)

    def between(s):
        if s in (3, 5, 7):
            mix_band((s - 3) // 2)

    sent_q = ring_gather(q_ref, qfull, qs, qr, between)
    sent += sent_q
    qfull[ds(z * 32, 32), :] = q_ref[...]
    mix_band(3)
    outs = [pltpu.make_async_copy(ab_ref, ab_hbm, lsem.at[0]), pltpu.make_async_copy(ac_ref, ac_hbm, lsem.at[1])]
    for copy in outs:
        copy.start()

    def product(side):
        band = ds(side * 128, 128)
        for n in range(2):
            part[band, 256 * n:256 * n + 256] = lax.dot_general(
                ab_ref[band, :], qfull[256 * n:256 * n + 256, :], (((1,), (1,)), ((), ())), preferred_element_type=F32
            )

    product(1 - core)
    swap = push(part.at[ds((1 - core) * 128, 128), :], rx1, cs, cr, tp=other)
    sent.append(swap)
    product(core)
    swap.wait_recv()
    half[...] = part[ds(core * 128, 128), :] + rx1[...]
    shares = []
    for d in (2, 1, 3):
        yd = lax.rem(y + d, Y)
        shares.append(push(half.at[ds(yd * 32, 32), :], rx2.at[d - 1], ys.at[d - 1], yr.at[d - 1], tp=yd * 2 + core))
    sent += shares
    for copy in shares:
        copy.wait_recv()
    p_ref[ds(core * 128 + y * 32, 32), :] = ((half[ds(y * 32, 32), :] + rx2[0]) + rx2[1]) + rx2[2]

    def pview(yy, cc, h):
        return p_ref.at[ds(cc * 128 + yy * 32 + 16 * h, 16), :]

    sent += y_gather(pview, True, ags, agr, aps, apr)
    gw[...] = lax.dot_general(
        p_ref[:, ds(y * 128, 128)], p_ref[...], (((0,), (0,)), ((), ())), precision=HI, preferred_element_type=F32
    )
    gp[...] = gw[ds(core * 64, 64), :]

    def piece(ref, base, zz):
        return ref.at[ds(base + 8 * (zz // 2), 8), ds(256 * lax.rem(zz, 2), 256)]

    pieces = []
    for d in range(1, Z):
        zz = lax.rem(z + d, Z)
        pieces.append(push(piece(gp, 0, zz), rg.at[d - 1], zs.at[d - 1], zr.at[d - 1], fsdp=zz))
    sent += pieces
    acc = gp[ds(8 * (z // 2), 8), ds(256 * lax.rem(z, 2), 256)]
    for d in range(1, Z):
        pieces[d - 1].wait_recv()
        acc = acc + rg[d - 1]
    base = y * 128 + core * 64
    g_ref[ds(base + 8 * (z // 2), 8), ds(256 * lax.rem(z, 2), 256)] = acc
    out = []
    for d in range(1, Z):
        zz = lax.rem(z + d, Z)
        out.append(push(piece(g_ref, base, z), piece(g_ref, base, z), gs.at[d - 1], gr.at[d - 1], fsdp=zz))
    sent += out
    for copy in out:
        copy.wait_recv()

    def gview(yy, cc, h):
        return g_ref.at[ds(yy * 128 + cc * 64 + 32 * h, 32), :]

    sent += y_gather(gview, True, hs, hr, hps, hpr)
    for copy in outs:
        copy.wait()
    for copy in sent:
        copy.wait_send()


VM = pl.BlockSpec(memory_space=pltpu.VMEM)
HB = pl.BlockSpec(memory_space=pltpu.HBM)
DMA = pltpu.SemaphoreType.DMA


def front(mix, tracker, grad, momentum, q_t):
    rows, cols = tracker.shape
    rank = q_t.shape[0] * Z
    sd = jax.ShapeDtypeStruct
    vm = pltpu.VMEM
    return pl.pallas_call(
        front_kernel,
        out_shape=(sd((rows, cols), BF), sd((rows, cols), BF), sd((rows, cols), F32), sd((rows, rank), F32), sd((rank, rank), F32)),
        in_specs=[pl.BlockSpec(memory_space=pltpu.SMEM)] + [HB] * 3 + [VM],
        out_specs=(VM, HB, HB, VM, VM),
        scratch_shapes=[
            vm((rows, cols), BF), vm((rows, cols), BF), vm((rows, cols), BF), vm((rows, cols), BF), vm((rows, cols), F32), DMA((3,)),
            vm((rows, cols), BF), vm((rows, cols), BF), vm((rank, cols), BF), vm((rows, rank), F32),
            vm((128, rank), F32), vm((128, rank), F32), vm((3, 32, rank), F32), vm((32, rank), F32),
            vm((128, rank), F32), vm((64, rank), F32), vm((15, 8, 256), F32),
            DMA((2, 4)), DMA((2, 4)), DMA((2, 8, 4)), DMA((2, 8, 4)), DMA, DMA, DMA((3,)), DMA((3,)),
            DMA((3, 2)), DMA((3, 2)), DMA((4, 2)), DMA((4, 2)),
            DMA((15,)), DMA((15,)), DMA((15,)), DMA((15,)),
            DMA((3, 2)), DMA((3, 2)), DMA((4, 2)), DMA((4, 2)),
        ],
        compiler_params=pltpu.CompilerParams(collective_id=0, has_side_effects=True, vmem_limit_bytes=67043328),
    )(mix, tracker, grad, momentum, q_t)


def back_kernel(lb_ref, ab_hbm, ac_hbm, qn_ref, nm_ref, ab_ref, ac_ref, lsem, lt, prod, sbuf, rbuf, rb, rfull, sq, sqr,
                rs, rr, gs, gr, ss, sr):
    me = lax.axis_index("fsdp")
    tp = lax.axis_index("tp")
    right, left = lax.rem(me + 1, Z), lax.rem(me + Z - 1, Z)
    peers = [lax.rem(tp + d, T) for d in range(1, T)]
    load_b = pltpu.make_async_copy(ab_hbm, ab_ref, lsem.at[0])
    load_a = pltpu.make_async_copy(ac_hbm, ac_ref, lsem.at[1])
    load_b.start()
    load_a.start()
    lt[...] = lb_ref[...].T
    enter([{"fsdp": right}, {"fsdp": left}] + [{"tp": t} for t in peers])
    cols = ab_ref.shape[1]
    wide = cols // 2
    scale = 1.0 / D ** 0.5
    load_b.wait()
    sent = []
    last = {}
    for s in range(Z // 2):
        if s == 0:
            far = jnp.dot(lt[ds(lax.rem(me + 8, Z) * 32, 32), :], ab_ref[...], preferred_element_type=F32) * scale
        for q in range(4):
            h, lanes = q // 2, slice((q % 2) * wide, (q % 2) * wide + wide)
            for way in range(2):
                if s == 0 and way != h:
                    continue
                rows = slice(16 * h, 16 * h + 16)
                if s == 0:
                    term = far[rows, lanes]
                else:
                    goal = lax.rem(me + 8 - s, Z) if way == 0 else lax.rem(me + Z - 8 + s, Z)
                    term = prod[ds(goal * 32 + 16 * h, 16), lanes]
                    if (q, way) in last:
                        last[q, way].wait_recv()
                        term = term + rbuf[way, s - 1, rows, lanes].astype(F32)
                sbuf[way, s, rows, lanes] = term.astype(BF)
                copy = push(
                    sbuf.at[way, s, rows, lanes], rbuf.at[way, s, rows, lanes],
                    rs.at[way, s, q], rr.at[way, s, q], fsdp=right if way == 0 else left,
                )
                last[q, way] = copy
                sent.append(copy)
        if s == 0:
            for n in range(cols // 256):
                part = slice(256 * n, 256 * n + 256)
                prod[:, part] = jnp.dot(lt[...], ab_ref[:, part], preferred_element_type=F32) * scale
    for copy in last.values():
        copy.wait_recv()
    mine = prod[ds(me * 32, 32), :] + rbuf[0, 7].astype(F32) + rbuf[1, 7].astype(F32)
    rb[...] = mine.astype(BF)
    rfull[ds(me * 32, 32), :] = mine.astype(BF)
    sq[...] = jnp.broadcast_to(jnp.sum(mine * mine, axis=1, keepdims=True), sq.shape)
    small = []
    for d in range(1, T):
        small.append(push(sq, sqr.at[d - 1], ss.at[d - 1], sr.at[d - 1], tp=peers[d - 1]))
    sent += small
    sent += ring_gather(rb, rfull, gs, gr)
    total = sq[...]
    for d in range(1, T):
        small[d - 1].wait_recv()
        total = total + sqr[d - 1]
    rms = jnp.sqrt(total / FF) + 1e-06
    qn_ref[...] = (mine / rms[:, 0:1]).astype(BF)
    load_a.wait()
    for n in range(cols // 256):
        part = slice(256 * n, 256 * n + 256)
        feed = jnp.dot(lb_ref[...], rfull[:, part], preferred_element_type=F32)
        nm_ref[:, part] = (ac_ref[:, part] - 0.5 * scale * feed).astype(BF)
    for copy in sent:
        copy.wait_send()


def back(left_b, accum_b, accum):
    rows, cols = accum.shape
    rank = left_b.shape[1]
    sd = jax.ShapeDtypeStruct
    vm = pltpu.VMEM
    return pl.pallas_call(
        back_kernel,
        out_shape=(sd((32, cols), BF), sd((rows, cols), BF)),
        in_specs=[VM, HB, HB],
        out_specs=(VM,) * 2,
        scratch_shapes=[
            vm((rows, cols), BF), vm((rows, cols), F32), DMA((2,)), vm((rank, rows), BF),
            vm((rank, cols), F32), vm((2, 8, 32, cols), BF), vm((2, 8, 32, cols), BF), vm((32, cols), BF),
            vm((rank, cols), BF), vm((32, 128), F32), vm((7, 32, 128), F32),
            DMA((2, 8, 4)), DMA((2, 8, 4)), DMA((2, 8, 4)), DMA((2, 8, 4)), DMA((7,)), DMA((7,)),
        ],
        compiler_params=pltpu.CompilerParams(collective_id=1, has_side_effects=True, vmem_limit_bytes=67043328),
    )(left_b, accum_b, accum)


def local(tracker, grad_delta, momentum, q_basis, mix_counts):
    new_tracker, accum_b, accum, pmat, gram = front(mix_counts, tracker[0], grad_delta[0], momentum[0], q_basis[0].T)
    left_b = left_solve(gram, pmat)
    q_t, new_momentum = back(left_b, accum_b, accum)
    return (new_tracker[None], new_momentum[None], left_b[None], q_t.T[None])


def solution(mesh):
    in_specs = (
        P("rep", "fsdp", "tp"),
        P("rep", "fsdp", "tp"),
        P("rep", "fsdp", "tp"),
        P("rep", "tp", "fsdp"),
        P(),
    )
    out_specs = (
        P("rep", "fsdp", "tp"),
        P("rep", "fsdp", "tp"),
        P("rep", "fsdp", None),
        P("rep", "tp", "fsdp"),
    )
    return jax.shard_map(local, mesh=mesh, in_specs=in_specs, out_specs=out_specs, check_vma=False)
```

```python
import jax
import jax.numpy as jnp
from jax import lax
from jax.experimental import pallas as pl
from jax.experimental.pallas import tpu as pltpu
from jax.sharding import PartitionSpec as P

D = 4096
FF = 14336


NB = 128
HI = lax.Precision.HIGHEST

def factor_inverse(load, store):
    G = NB // 8
    sub = lax.broadcasted_iota(jnp.int32, (8, NB), 0)
    lane = lax.broadcasted_iota(jnp.int32, (8, NB), 1)
    A = [load(h) for h in range(G)]
    W = [jnp.where(lane == sub + 8 * h, 1.0, 0.0).astype(jnp.float32) for h in range(G)]
    row = lambda x, a: jnp.broadcast_to(x[a:a + 1, :], (8, NB))
    colb = lambda x, j: jnp.broadcast_to(x[:, j:j + 1], (8, NB))
    for g in range(G):
        j0 = 8 * g
        RA, RW = A[g], W[g]
        E = [colb(RA, j0 + a) for a in range(8)]
        FA, FW = RA, RW
        for a in range(8):
            ra, rw = row(RA, a), row(RW, a)
            inv = 1.0 / row(E[a], a)
            hit = sub == a
            FA = jnp.where(hit, ra, FA)
            FW = jnp.where(hit, rw, FW)
            sa, sw = ra * inv, rw * inv
            RA = jnp.where(hit, sa, RA - E[a] * sa)
            RW = jnp.where(hit, sw, RW - E[a] * sw)
            for b in range(a + 1, 8):
                eb = row(E[b], a) * inv
                E[b] = jnp.where(hit, eb, E[b] - E[a] * eb)
        A[g], W[g] = FA, FW
        SA = [row(RA, a) for a in range(8)]
        SW = [row(RW, a) for a in range(8)]
        for h in range(g + 1, G):
            ah, wh, src = A[h], W[h], A[h]
            for a in range(8):
                c = colb(src, j0 + a)
                ah = ah - c * SA[a]
                wh = wh - c * SW[a]
            A[h], W[h] = ah, wh
    for g in range(G):
        d = jnp.sum(jnp.where(lane == sub + 8 * g, A[g], 0.0), axis=1, keepdims=True)
        store(g, W[g] * lax.rsqrt(d))

def nt(a, b):
    return lax.dot_general(a, b, (((1,), (1,)), ((), ())), precision=HI, preferred_element_type=jnp.float32)

def split(x):
    high = x.astype(jnp.bfloat16)
    return high, (x - high.astype(jnp.float32)).astype(jnp.bfloat16)


def nt_split(a, b):
    (ah, al), (bh, bl) = split(a), split(b)
    one = lambda x, y: lax.dot_general(x, y, (((1,), (1,)), ((), ())), preferred_element_type=jnp.float32)
    return one(ah, bh) + (one(ah, bl) + one(al, bh))


def solve_kernel(g_ref, p_ref, nt_hbm, o_ref, nt_out, t_ref, w_ref, stage, sem):
    n = g_ref.shape[0]
    fetch = pltpu.make_async_copy(nt_hbm, stage, sem.at[0])
    flush = pltpu.make_async_copy(stage, nt_out, sem.at[1])
    fetch.start()
    m = p_ref.shape[0]
    K = n // NB
    t_ref[0:n, :] = g_ref[...]
    t_ref[n:n + m, :] = p_ref[...]
    def step(k, _):
        base = pl.multiple_of(k * NB, NB)
        def load(h):
            return t_ref[pl.ds(pl.multiple_of(base + 8 * h, 8), 8), pl.ds(base, NB)]
        def store(h, v):
            w_ref[8 * h:8 * h + 8, :] = v
        factor_inverse(load, store)
        for kk in range(K):
            @pl.when(k == kk)
            def _():
                if kk == 1:
                    fetch.wait()
                    flush.start()
                lo, hi = kk * NB, (kk + 1) * NB
                y = nt_split(t_ref[n:, lo:hi], w_ref[...])
                o_ref[:, lo:hi] = (y * D ** 0.5).astype(jnp.bfloat16)
                if kk + 1 < K:
                    x = nt(t_ref[hi:n, lo:hi], w_ref[...])
                    t_ref[hi:n, hi:] = t_ref[hi:n, hi:] - nt(x, x)
                    t_ref[n:, hi:] = t_ref[n:, hi:] - nt_split(y, x)
        return 0
    lax.fori_loop(0, K, step, 0)
    flush.wait()

def left_solve(gram, pmat, tracker):
    n, m = gram.shape[0], pmat.shape[0]
    return pl.pallas_call(
        solve_kernel,
        out_shape=(jax.ShapeDtypeStruct((m, n), jnp.bfloat16), jax.ShapeDtypeStruct(tracker.shape, jnp.bfloat16)),
        in_specs=[pl.BlockSpec(memory_space=pltpu.VMEM)] * 2 + [pl.BlockSpec(memory_space=pltpu.HBM)],
        out_specs=(pl.BlockSpec(memory_space=pltpu.VMEM), pl.BlockSpec(memory_space=pltpu.HBM)),
        scratch_shapes=[pltpu.VMEM((n + m, n), jnp.float32), pltpu.VMEM((NB, NB), jnp.float32),
                        pltpu.VMEM(tracker.shape, jnp.bfloat16), pltpu.SemaphoreType.DMA((2,))],
        compiler_params=pltpu.CompilerParams(vmem_limit_bytes=67043328),
    )(gram, pmat, tracker)


MESH = pl.DeviceIdType.MESH
Z, Y, T = 16, 4, 8
BF = jnp.bfloat16
F32 = jnp.float32


def ds(start, size):
    return pl.ds(pl.multiple_of(start, size), size)


def push(src, dst, ssem, rsem, **where):
    copy = pltpu.make_async_remote_copy(
        src_ref=src, dst_ref=dst, send_sem=ssem, recv_sem=rsem, device_id=where, device_id_type=MESH
    )
    copy.start()
    return copy


def enter(peers):
    barrier = pltpu.get_barrier_semaphore()
    for where in peers:
        pl.semaphore_signal(barrier, inc=1, device_id=where, device_id_type=MESH)
    pl.semaphore_wait(barrier, len(peers))


def ring_gather(first, full, ssem, rsem, between=None):
    me = lax.axis_index("fsdp")
    right, left = lax.rem(me + 1, Z), lax.rem(me + Z - 1, Z)
    wide = first.shape[1] // 2
    sent = []
    last = {}
    for s in range(Z // 2):
        for q in range(4):
            h, lanes = q // 2, slice((q % 2) * wide, (q % 2) * wide + wide)
            for way in range(2):
                if s == Z // 2 - 1 and way != h:
                    continue
                owner = lax.rem(me - s + Z, Z) if way == 0 else lax.rem(me + s, Z)
                dst = full.at[ds(owner * 32 + 16 * h, 16), lanes]
                if s > 0:
                    last[q, way].wait_recv()
                src = first.at[16 * h:16 * h + 16, lanes] if s == 0 else dst
                copy = push(src, dst, ssem.at[way, s, q], rsem.at[way, s, q], fsdp=right if way == 0 else left)
                last[q, way] = copy
                sent.append(copy)
        if between is not None:
            between(s)
    for copy in last.values():
        copy.wait_recv()
    return sent


def y_gather(view, partner_too, ssem, rsem, psend, precv):
    tp = lax.axis_index("tp")
    y, core = tp // 2, lax.rem(tp, 2)
    other = tp + 1 - 2 * core
    up, down, far = lax.rem(y + 1, Y), lax.rem(y + Y - 1, Y), lax.rem(y + 2, Y)
    sent = []
    cross = []
    halves = {}
    for h in range(2):
        for way, goal in ((0, up), (1, down)):
            copy = push(view(y, core, h), view(y, core, h), ssem.at[way, h], rsem.at[way, h], tp=goal * 2 + core)
            halves[way, h] = copy
            sent.append(copy)
    for h in range(2):
        cross.append(push(view(y, core, h), view(y, core, h), psend.at[0, h], precv.at[0, h], tp=other))
    for h in (0, 1):
        way = h
        origin, goal = (down, up) if way == 0 else (up, down)
        halves[way, h].wait_recv()
        copy = push(view(origin, core, h), view(origin, core, h), ssem.at[2, h], rsem.at[2, h], tp=goal * 2 + core)
        halves[2, h] = copy
        sent.append(copy)
        cross.append(push(view(origin, core, h), view(origin, core, h), psend.at[1 + way, h], precv.at[1 + way, h], tp=other))
    for way, h in ((0, 1), (1, 0)):
        origin = down if way == 0 else up
        halves[way, h].wait_recv()
        cross.append(push(view(origin, core, h), view(origin, core, h), psend.at[1 + way, h], precv.at[1 + way, h], tp=other))
    for h in range(2):
        halves[2, h].wait_recv()
        cross.append(push(view(far, core, h), view(far, core, h), psend.at[3, h], precv.at[3, h], tp=other))
    for copy in cross:
        copy.wait_recv()
    return sent + cross


def front_kernel(mix_ref, tr_hbm, gd_hbm, mo_hbm, q_ref, nt_ref, ab_hbm, ac_hbm, p_ref, g_ref,
                 tr_ref, gd_ref, mo_ref, ab_ref, ac_ref, lsem, tlo, thi, qfull, part, rx1, half, rx2, own, gw, gp, rg,
                 xs, xr, qs, qr, cs, cr, ys, yr, ags, agr, aps, apr, zs, zr, gs, gr, hs, hr, hps, hpr):
    x = lax.axis_index("rep")
    z = lax.axis_index("fsdp")
    tp = lax.axis_index("tp")
    y, core = tp // 2, lax.rem(tp, 2)
    other = tp + 1 - 2 * core
    xn = lax.axis_size("rep")
    xu, xd = lax.rem(x + 1, xn), lax.rem(x + xn - 1, xn)
    zu, zd = lax.rem(z + 1, Z), lax.rem(z + Z - 1, Z)
    ypeers = [lax.rem(y + d, Y) * 2 + core for d in range(1, Y)]
    loads = [
        pltpu.make_async_copy(src, dst, lsem.at[i])
        for i, (src, dst) in enumerate(((tr_hbm, tr_ref), (gd_hbm, gd_ref), (mo_hbm, mo_ref)))
    ]
    for copy in loads:
        copy.start()
    enter([{"rep": xu}, {"rep": xd}, {"fsdp": zu}, {"fsdp": zd}, {"tp": other}] + [{"tp": t} for t in ypeers])
    sent = []
    arrivals = []
    for k in range(4):
        band = slice(64 * k, 64 * k + 64)
        up = push(tr_hbm.at[band], tlo.at[band], xs.at[0, k], xr.at[0, k], rep=xu)
        down = push(tr_hbm.at[band], thi.at[band], xs.at[1, k], xr.at[1, k], rep=xd)
        arrivals.append((up, down))
        sent += [up, down]
    c = [jnp.full((8, 128), mix_ref[x, i].astype(F32)) for i in range(3)]
    total = c[0] + c[1] + c[2]
    w = [(v / total)[0:1, 0:1] for v in c]

    def mixing(i, _):
        r = ds(i * 16, 16)
        tracked = (
            w[0] * tr_ref[r, :].astype(F32) + w[1] * tlo[r, :].astype(F32) + w[2] * thi[r, :].astype(F32)
        ) + gd_ref[r, :].astype(F32)
        accum = mo_ref[r, :].astype(F32) + tracked
        nt_ref[r, :] = tracked.astype(BF)
        ac_ref[r, :] = accum
        ab_ref[r, :] = accum.astype(BF)
        return 0

    def mix_band(k):
        if k == 0:
            for copy in loads:
                copy.wait()
        for copy in arrivals[k]:
            copy.wait_recv()
        lax.fori_loop(4 * k, 4 * k + 4, mixing, 0)

    def between(s):
        if s in (3, 5, 7):
            mix_band((s - 3) // 2)

    sent_q = ring_gather(q_ref, qfull, qs, qr, between)
    sent += sent_q
    qfull[ds(z * 32, 32), :] = q_ref[...]
    mix_band(3)
    outs = [pltpu.make_async_copy(ab_ref, ab_hbm, lsem.at[0]), pltpu.make_async_copy(ac_ref, ac_hbm, lsem.at[1])]
    for copy in outs:
        copy.start()

    def product(side):
        band = ds(side * 128, 128)
        for n in range(2):
            part[band, 256 * n:256 * n + 256] = lax.dot_general(
                ab_ref[band, :], qfull[256 * n:256 * n + 256, :], (((1,), (1,)), ((), ())), preferred_element_type=F32
            )

    product(1 - core)
    swap = push(part.at[ds((1 - core) * 128, 128), :], rx1, cs, cr, tp=other)
    sent.append(swap)
    product(core)
    swap.wait_recv()
    half[...] = part[ds(core * 128, 128), :] + rx1[...]
    shares = []
    for d in (2, 1, 3):
        yd = lax.rem(y + d, Y)
        shares.append(push(half.at[ds(yd * 32, 32), :], rx2.at[d - 1], ys.at[d - 1], yr.at[d - 1], tp=yd * 2 + core))
    sent += shares
    for copy in shares:
        copy.wait_recv()
    p_ref[ds(core * 128 + y * 32, 32), :] = ((half[ds(y * 32, 32), :] + rx2[0]) + rx2[1]) + rx2[2]

    def pview(yy, cc, h):
        return p_ref.at[ds(cc * 128 + yy * 32 + 16 * h, 16), :]

    sent += y_gather(pview, True, ags, agr, aps, apr)
    gw[...] = lax.dot_general(
        p_ref[:, ds(y * 128, 128)], p_ref[...], (((0,), (0,)), ((), ())), precision=HI, preferred_element_type=F32
    )
    gp[...] = gw[ds(core * 64, 64), :]

    def piece(ref, base, zz):
        return ref.at[ds(base + 8 * (zz // 2), 8), ds(256 * lax.rem(zz, 2), 256)]

    pieces = []
    for d in range(1, Z):
        zz = lax.rem(z + d, Z)
        pieces.append(push(piece(gp, 0, zz), rg.at[d - 1], zs.at[d - 1], zr.at[d - 1], fsdp=zz))
    sent += pieces
    acc = gp[ds(8 * (z // 2), 8), ds(256 * lax.rem(z, 2), 256)]
    for d in range(1, Z):
        pieces[d - 1].wait_recv()
        acc = acc + rg[d - 1]
    base = y * 128 + core * 64
    g_ref[ds(base + 8 * (z // 2), 8), ds(256 * lax.rem(z, 2), 256)] = acc
    out = []
    for d in range(1, Z):
        zz = lax.rem(z + d, Z)
        out.append(push(piece(g_ref, base, z), piece(g_ref, base, z), gs.at[d - 1], gr.at[d - 1], fsdp=zz))
    sent += out
    for copy in out:
        copy.wait_recv()

    def gview(yy, cc, h):
        return g_ref.at[ds(yy * 128 + cc * 64 + 32 * h, 32), :]

    sent += y_gather(gview, True, hs, hr, hps, hpr)
    for copy in outs:
        copy.wait()
    for copy in sent:
        copy.wait_send()


VM = pl.BlockSpec(memory_space=pltpu.VMEM)
HB = pl.BlockSpec(memory_space=pltpu.HBM)
DMA = pltpu.SemaphoreType.DMA


def front(mix, tracker, grad, momentum, q_t):
    rows, cols = tracker.shape
    rank = q_t.shape[0] * Z
    sd = jax.ShapeDtypeStruct
    vm = pltpu.VMEM
    return pl.pallas_call(
        front_kernel,
        out_shape=(sd((rows, cols), BF), sd((rows, cols), BF), sd((rows, cols), F32), sd((rows, rank), F32), sd((rank, rank), F32)),
        in_specs=[pl.BlockSpec(memory_space=pltpu.SMEM)] + [HB] * 3 + [VM],
        out_specs=(VM, HB, HB, VM, VM),
        scratch_shapes=[
            vm((rows, cols), BF), vm((rows, cols), BF), vm((rows, cols), BF), vm((rows, cols), BF), vm((rows, cols), F32), DMA((3,)),
            vm((rows, cols), BF), vm((rows, cols), BF), vm((rank, cols), BF), vm((rows, rank), F32),
            vm((128, rank), F32), vm((128, rank), F32), vm((3, 32, rank), F32), vm((32, rank), F32),
            vm((128, rank), F32), vm((64, rank), F32), vm((15, 8, 256), F32),
            DMA((2, 4)), DMA((2, 4)), DMA((2, 8, 4)), DMA((2, 8, 4)), DMA, DMA, DMA((3,)), DMA((3,)),
            DMA((3, 2)), DMA((3, 2)), DMA((4, 2)), DMA((4, 2)),
            DMA((15,)), DMA((15,)), DMA((15,)), DMA((15,)),
            DMA((3, 2)), DMA((3, 2)), DMA((4, 2)), DMA((4, 2)),
        ],
        compiler_params=pltpu.CompilerParams(collective_id=0, has_side_effects=True, vmem_limit_bytes=67043328),
    )(mix, tracker, grad, momentum, q_t)


def back_kernel(lb_ref, ab_hbm, ac_hbm, qn_ref, nm_ref, ab_ref, ac_ref, lsem, lt, prod, sbuf, rbuf, rb, rfull, sq, sqr,
                rs, rr, gs, gr, ss, sr):
    me = lax.axis_index("fsdp")
    tp = lax.axis_index("tp")
    right, left = lax.rem(me + 1, Z), lax.rem(me + Z - 1, Z)
    peers = [lax.rem(tp + d, T) for d in range(1, T)]
    load_b = pltpu.make_async_copy(ab_hbm, ab_ref, lsem.at[0])
    load_a = pltpu.make_async_copy(ac_hbm, ac_ref, lsem.at[1])
    load_b.start()
    load_a.start()
    lt[...] = lb_ref[...].T
    enter([{"fsdp": right}, {"fsdp": left}] + [{"tp": t} for t in peers])
    cols = ab_ref.shape[1]
    wide = cols // 2
    scale = 1.0 / D ** 0.5
    load_b.wait()
    sent = []
    last = {}
    for s in range(Z // 2):
        if s == 0:
            far = jnp.dot(lt[ds(lax.rem(me + 8, Z) * 32, 32), :], ab_ref[...], preferred_element_type=F32) * scale
        for q in range(4):
            h, lanes = q // 2, slice((q % 2) * wide, (q % 2) * wide + wide)
            for way in range(2):
                if s == 0 and way != h:
                    continue
                rows = slice(16 * h, 16 * h + 16)
                if s == 0:
                    term = far[rows, lanes]
                else:
                    goal = lax.rem(me + 8 - s, Z) if way == 0 else lax.rem(me + Z - 8 + s, Z)
                    term = prod[ds(goal * 32 + 16 * h, 16), lanes]
                    if (q, way) in last:
                        last[q, way].wait_recv()
                        term = term + rbuf[way, s - 1, rows, lanes].astype(F32)
                sbuf[way, s, rows, lanes] = term.astype(BF)
                copy = push(
                    sbuf.at[way, s, rows, lanes], rbuf.at[way, s, rows, lanes],
                    rs.at[way, s, q], rr.at[way, s, q], fsdp=right if way == 0 else left,
                )
                last[q, way] = copy
                sent.append(copy)
        if s == 0:
            for n in range(cols // 256):
                part = slice(256 * n, 256 * n + 256)
                prod[:, part] = jnp.dot(lt[...], ab_ref[:, part], preferred_element_type=F32) * scale
    for copy in last.values():
        copy.wait_recv()
    mine = prod[ds(me * 32, 32), :] + rbuf[0, 7].astype(F32) + rbuf[1, 7].astype(F32)
    rb[...] = mine.astype(BF)
    rfull[ds(me * 32, 32), :] = mine.astype(BF)
    sq[...] = jnp.broadcast_to(jnp.sum(mine * mine, axis=1, keepdims=True), sq.shape)
    small = []
    for d in range(1, T):
        small.append(push(sq, sqr.at[d - 1], ss.at[d - 1], sr.at[d - 1], tp=peers[d - 1]))
    sent += small
    sent += ring_gather(rb, rfull, gs, gr)
    total = sq[...]
    for d in range(1, T):
        small[d - 1].wait_recv()
        total = total + sqr[d - 1]
    rms = jnp.sqrt(total / FF) + 1e-06
    qn_ref[...] = (mine / rms[:, 0:1]).astype(BF)
    load_a.wait()
    for n in range(cols // 256):
        part = slice(256 * n, 256 * n + 256)
        feed = jnp.dot(lb_ref[...], rfull[:, part], preferred_element_type=F32)
        nm_ref[:, part] = (ac_ref[:, part] - 0.5 * scale * feed).astype(BF)
    for copy in sent:
        copy.wait_send()


def back(left_b, accum_b, accum):
    rows, cols = accum.shape
    rank = left_b.shape[1]
    sd = jax.ShapeDtypeStruct
    vm = pltpu.VMEM
    return pl.pallas_call(
        back_kernel,
        out_shape=(sd((32, cols), BF), sd((rows, cols), BF)),
        in_specs=[VM, HB, HB],
        out_specs=(VM,) * 2,
        scratch_shapes=[
            vm((rows, cols), BF), vm((rows, cols), F32), DMA((2,)), vm((rank, rows), BF),
            vm((rank, cols), F32), vm((2, 8, 32, cols), BF), vm((2, 8, 32, cols), BF), vm((32, cols), BF),
            vm((rank, cols), BF), vm((32, 128), F32), vm((7, 32, 128), F32),
            DMA((2, 8, 4)), DMA((2, 8, 4)), DMA((2, 8, 4)), DMA((2, 8, 4)), DMA((7,)), DMA((7,)),
        ],
        compiler_params=pltpu.CompilerParams(collective_id=1, has_side_effects=True, vmem_limit_bytes=67043328),
    )(left_b, accum_b, accum)


def local(tracker, grad_delta, momentum, q_basis, mix_counts):
    new_tracker, accum_b, accum, pmat, gram = front(mix_counts, tracker[0], grad_delta[0], momentum[0], q_basis[0].T)
    left_b, new_tracker = left_solve(gram, pmat, new_tracker)
    q_t, new_momentum = back(left_b, accum_b, accum)
    return (new_tracker[None], new_momentum[None], left_b[None], q_t.T[None])


def solution(mesh):
    in_specs = (
        P("rep", "fsdp", "tp"),
        P("rep", "fsdp", "tp"),
        P("rep", "fsdp", "tp"),
        P("rep", "tp", "fsdp"),
        P(),
    )
    out_specs = (
        P("rep", "fsdp", "tp"),
        P("rep", "fsdp", "tp"),
        P("rep", "fsdp", None),
        P("rep", "tp", "fsdp"),
    )
    return jax.shard_map(local, mesh=mesh, in_specs=in_specs, out_specs=out_specs, check_vma=False)
```
